32 devices in a mesh: energy: 4 (over y, x), kmom: 8 (over z, core).
Axes of the slice: x: 2, y: 2, z: 4, core: 2. Of those that a mesh axis runs over, the one named last changes fastest.
Arguments:
- green_blocks: bfloat16 [8, 8, 144, 1024], P('energy', 'kmom'), may hold values from -6 to 6
- phonon: float32 [2, 8, 8], replicated, may hold values from -0.4 to 0.4
- offsets: int32 [8], replicated, may hold values from 1 to 2, as said below
- neighbours: int32 [1024, 8], P('kmom'), may hold values from 0 to 1023, as said below
- coupling: float32 [8, 12, 12], replicated, may hold values from -1.75 to 1.75
Outputs:
- self_energy: bfloat16 [8, 8, 144, 1024], P('energy', 'kmom')
The draws below stay inside these ranges and needn't reach their ends.
Inputs may be any that keep to these rules, and one draw needn't show every extreme that they name: `offsets`: each value lies in 1 .. 2; at least one equals 2. Every neighbour of atom a lies within 32 of a in index; some atom has neighbours at exactly a + 32 and a - 32.
All inputs are finite; a program needn't handle non-finite values.
Results may differ from the reference program's by a relative error of at most 0.0064.
Values may be sent and summed in bfloat16 or wider, within the bound.
A program may use at most 64 MiB of HBM per device.

```python
import jax
import jax.numpy as jnp
from jax import lax

NORB = 12
NPAIR = 144
NW = 8
NB = 8
NK = 8
E_DEV = 2
OFFSET = 2
RADIUS = 32
NE = 8
NA = 1024


def draw_offsets(key, part):
    base_values = jax.random.randint(key, (NW,), 1, OFFSET + 1, dtype=jnp.int32)
    chosen = jax.random.randint(jax.random.fold_in(key, 7), (), 0, NW, dtype=jnp.int32)
    places = jnp.arange(NW, dtype=jnp.int32)
    return jnp.where(places == chosen, OFFSET, base_values).astype(jnp.int32)


def draw_neighbours(key, part):
    steps_drawn = jax.random.randint(key, (NA, NB), -RADIUS, RADIUS + 1, dtype=jnp.int32)
    chosen = jax.random.randint(jax.random.fold_in(key, 11), (), RADIUS, NA - RADIUS, dtype=jnp.int32)
    atom_ids = jnp.arange(NA, dtype=jnp.int32)[:, None]
    slot_ids = jnp.arange(NB, dtype=jnp.int32)[None, :]
    steps_drawn = jnp.where((atom_ids == chosen) & (slot_ids == 0), RADIUS, steps_drawn)
    steps_drawn = jnp.where((atom_ids == chosen) & (slot_ids == 1), -RADIUS, steps_drawn)
    return jnp.clip(atom_ids + steps_drawn, 0, NA - 1).astype(jnp.int32)


def steps_of(rng, extent, pieces, least, top_value):
    factor_of, own = 1.0, jax.random.fold_in(rng, 6)
    for axis_at, parts in pieces:
        draws = jnp.exp(jax.random.uniform(jax.random.fold_in(own, axis_at), (parts,), jnp.float32, least / len(pieces), top_value / len(pieces)))
        factor_of = factor_of * jnp.repeat(draws, extent[axis_at] // parts).reshape([-1 if axis == axis_at else 1 for axis in range(len(extent))])
    return factor_of


def scatter_about(rng, shape, deviation, bound, shards=(), kind=jnp.bfloat16):
    entries = deviation * jax.random.normal(rng, shape, jnp.float32)
    if shards:
        entries = entries * steps_of(rng, shape, shards, -0.22, 0.18)
    return jnp.clip(entries, -bound, bound).astype(kind)


def setup_inputs(seed: int = 0) -> dict:
    seeds = jax.random.split(jax.random.key(seed), 6)
    green_blocks = scatter_about(seeds[0], (NE, NK, NPAIR, NA), 1.0, 6.0, ((0, 4), (1, 8)))
    phonon = scatter_about(seeds[1], (2, NW, NK), 0.0625, 0.4, (), jnp.float32)
    offsets = draw_offsets(jax.random.fold_in(seeds[5], 71), 0)
    neighbours = draw_neighbours(jax.random.fold_in(seeds[5], 71), 0)
    coupling = scatter_about(seeds[4], (NB, NORB, NORB), NORB ** -0.5, 1.75, (), jnp.float32)
    return dict(green_blocks=green_blocks, phonon=phonon, offsets=offsets, neighbours=neighbours, coupling=coupling)


def energy_kernel(phonon, offsets, block_rows):
    mom_count = phonon.shape[2]
    rel_values = jnp.arange(2 * OFFSET + 1, dtype=jnp.int32) - OFFSET
    sign_values = jnp.array([-1, 1], dtype=jnp.int32)
    shifts = sign_values[:, None] * offsets[None, :]
    rel_hit = (shifts[:, :, None] == rel_values[None, None, :]).astype(jnp.float32)
    energy_taps = jnp.einsum("swr,swq->rq", rel_hit, phonon.astype(jnp.float32), precision=lax.Precision.HIGHEST)
    energy_taps = energy_taps.astype(jnp.bfloat16).astype(jnp.float32)
    out_rows = jnp.arange(block_rows, dtype=jnp.int32)
    in_rows = jnp.arange(block_rows + 2 * OFFSET, dtype=jnp.int32)
    tap_index = jnp.arange(2 * OFFSET + 1, dtype=jnp.int32)
    row_hit = ((in_rows[None, :, None] - out_rows[:, None, None]) == tap_index[None, None, :]).astype(jnp.float32)
    moms = jnp.arange(mom_count, dtype=jnp.int32)
    mom_hit = (((moms[:, None, None] - moms[None, :, None]) % mom_count) == moms[None, None, :]).astype(jnp.float32)
    kernel = jnp.einsum("abr,kjq,rq->akbj", row_hit, mom_hit, energy_taps, precision=lax.Precision.HIGHEST)
    kernel = kernel.reshape(block_rows * mom_count, (block_rows + 2 * OFFSET) * mom_count)
    return kernel.astype(jnp.bfloat16)


def orbital_pairs(coupling):
    slots = coupling.shape[0]
    orbs = coupling.shape[1]
    outer = jnp.einsum("nip,njr->nijpr", coupling, coupling, precision=lax.Precision.HIGHEST)
    return outer.reshape(slots, orbs * orbs, orbs * orbs).astype(jnp.bfloat16)


def reference(green_blocks, phonon, offsets, neighbours, coupling):
    kernel = energy_kernel(phonon, offsets, E_DEV)
    pair_maps = orbital_pairs(coupling)

    def one_energy(green_row):
        def add_slot(running, scan_item):
            near_atoms, pair_map = scan_item
            taken = jnp.take(green_row, near_atoms, axis=2)
            product = jnp.einsum("kca,dc->kda", taken.astype(jnp.float32), pair_map.astype(jnp.float32))
            return running + product, None

        start_sum = jnp.zeros((NK, NPAIR, NA), jnp.float32)
        running, _ = lax.scan(add_slot, start_sum, (neighbours.T, pair_maps))
        return running.astype(jnp.bfloat16)

    coupled = lax.map(one_energy, green_blocks)
    padded = jnp.pad(coupled, ((OFFSET, OFFSET), (0, 0), (0, 0), (0, 0)))
    tiles = NE // E_DEV

    def one_tile(tile_index):
        first_row = (tile_index * E_DEV).astype(jnp.int32)
        window = lax.dynamic_slice_in_dim(padded, first_row, E_DEV + 2 * OFFSET, 0)
        flat_window = window.reshape((E_DEV + 2 * OFFSET) * NK, NPAIR * NA)
        smeared = jnp.dot(kernel, flat_window, preferred_element_type=jnp.float32).astype(jnp.bfloat16)
        return smeared.reshape(E_DEV, NK, NPAIR, NA)

    result = lax.map(one_tile, jnp.arange(tiles, dtype=jnp.int32))
    return result.reshape(NE, NK, NPAIR, NA)
```

```python
import functools

import jax
import jax.numpy as jnp
import numpy as np
from jax import lax
from jax.experimental import pallas as pl
from jax.experimental.pallas import tpu as pltpu
from jax.sharding import PartitionSpec as P

OFFSET = 2
RADIUS = 32
ROWS = 16
EARLY = 7
MESH = pl.DeviceIdType.MESH


def spread_ones(slots, orbs):
    col = np.arange(slots * orbs * orbs)
    row = np.arange(slots * orbs)[:, None]
    first = row == col // orbs
    second = row == (col // (orbs * orbs)) * orbs + col % orbs
    return jnp.asarray(np.concatenate([first, second], axis=1), jnp.bfloat16)


def fill_maps(coupling, ones, maps_wide, maps):
    orbs, slots = coupling.shape[0], coupling.shape[1]
    count = slots * orbs * orbs
    blocks = jnp.concatenate([coupling[:, slot, :] for slot in range(slots)], axis=1)
    high = blocks.astype(jnp.bfloat16)
    rest = blocks - high.astype(jnp.float32)
    mid = rest.astype(jnp.bfloat16)
    low = (rest - mid.astype(jnp.float32)).astype(jnp.bfloat16)
    both = sum(
        jnp.dot(term, ones[...], preferred_element_type=jnp.float32) for term in (high, mid, low)
    )
    left, right = both[:, :count], both[:, count:]
    for orb in range(orbs):
        maps_wide[orb * orbs : (orb + 1) * orbs, :] = left[orb : orb + 1, :] * right
    maps[...] = maps_wide[...].astype(jnp.bfloat16)


def small_kernel(phonon, offsets, block_rows):
    freqs, moms = phonon.shape[1], phonon.shape[2]
    flat = moms * block_rows
    place = lax.broadcasted_iota(jnp.int32, (freqs, moms), 0)
    shift = jnp.zeros((freqs, moms), jnp.int32)
    for freq in range(freqs):
        shift = jnp.where(place == freq, offsets[freq], shift)
    row = lax.broadcasted_iota(jnp.int32, (flat, 3 * flat), 0)
    col = lax.broadcasted_iota(jnp.int32, (flat, 3 * flat), 1)
    mom_diff = (row // block_rows - (col // block_rows) % moms + moms) % moms
    tile = (col >= flat).astype(jnp.int32) + (col >= 2 * flat).astype(jnp.int32)
    rel = block_rows * (tile - 1) + col % block_rows - row % block_rows
    small = jnp.zeros((flat, 3 * flat), jnp.float32)
    for step in range(-OFFSET, OFFSET + 1):
        terms = [
            jnp.where((2 * sign - 1) * shift == step, phonon[sign], 0.0) for sign in (0, 1)
        ]
        taps = jnp.sum(terms[0] + terms[1], axis=0, keepdims=True)
        code = jnp.where(rel == step, mom_diff, -1)
        for mom in range(moms):
            small = jnp.where(code == mom, taps[:, mom : mom + 1], small)
    return small.astype(jnp.bfloat16)


def fill_wide(small, wide):
    flat = small.shape[0]
    grow = (
        lax.broadcasted_iota(jnp.int32, (flat * ROWS, flat), 0) // ROWS
        == lax.broadcasted_iota(jnp.int32, (flat * ROWS, flat), 1)
    )
    tall = jnp.dot(
        jnp.where(grow, 1.0, 0.0).astype(jnp.bfloat16), small, preferred_element_type=jnp.float32
    ).astype(jnp.bfloat16)
    for part in range(3):
        span = flat * ROWS
        spread = (
            lax.broadcasted_iota(jnp.int32, (flat, span), 1) // ROWS
            == lax.broadcasted_iota(jnp.int32, (flat, span), 0)
        )
        full = jnp.dot(
            tall[:, part * flat : (part + 1) * flat],
            jnp.where(spread, 1.0, 0.0).astype(jnp.bfloat16),
            preferred_element_type=jnp.float32,
        )
        same = (
            lax.broadcasted_iota(jnp.int32, (span, span), 0) % ROWS
            == lax.broadcasted_iota(jnp.int32, (span, span), 1) % ROWS
        )
        wide[:, part * span : (part + 1) * span] = jnp.where(same, full, 0.0).astype(jnp.bfloat16)


def SCOPE(name, act):
    with jax.named_scope(name):
        act()


def paired(index, step, count):
    if count & (count - 1):
        return lax.rem(index + step, count)
    total = jnp.int32(0)
    bit = 1
    while bit < count:
        total = total + lax.rem(lax.div(index, bit) + lax.div(step, bit), 2) * bit
        bit *= 2
    return total


def kernel(
    sizes, green_any, near_any, phonon_any, offsets_any, coupling_any, ones_any, out,
    green, near, phonon, offsets, coupling, ones, maps_wide, maps, near_all, taken, coupled, wide, recv, res,
    load_sem, near_send, near_recv, in_send, in_recv, out_send, out_recv,
):
    ne, nk, window = sizes
    block_rows, pairs, atoms = green.shape
    slots, group = near.shape
    tiles = pairs // ROWS
    rounds = recv.shape[0]
    my_e = lax.axis_index("energy")
    my_k = lax.axis_index("kmom")

    barrier = pltpu.get_barrier_semaphore()
    loads = [
        pltpu.make_async_copy(src, dst, load_sem.at[i])
        for i, (src, dst) in enumerate(
            [
                (coupling_any, coupling), (ones_any, ones), (near_any, near), (green_any, green),
                (phonon_any, phonon), (offsets_any, offsets),
            ]
        )
    ]
    for load in loads[:2]:
        load.start()

    def greet(i, _):
        place = lax.rem(my_e * nk + my_k + i, ne * nk)
        pl.semaphore_signal(
            barrier, inc=1, device_id=(lax.div(place, nk), lax.rem(place, nk)), device_id_type=MESH
        )
        return 0

    SCOPE("greet", lambda: lax.fori_loop(1, ne * nk, greet, 0))
    for load in loads[2:]:
        load.start()
    SCOPE("lones", lambda: [loads[0].wait(), loads[1].wait()])
    SCOPE("maps", lambda: fill_maps(coupling, ones, maps_wide, maps))
    flat = nk * block_rows

    def near_copy(i):
        other = paired(my_k, i, nk)
        return pltpu.make_async_remote_copy(
            src_ref=near, dst_ref=near_all.at[my_k], send_sem=near_send, recv_sem=near_recv.at[my_k],
            device_id=(my_e, other), device_id_type=MESH,
        )

    def all_others(act):
        def step(i, _):
            act(i)
            return 0

        lax.fori_loop(1, nk, step, 0)

    def in_copies(tile, grp, start):
        turn, step = tile // ne, tile % ne
        count = min(ne, tiles - turn * ne)
        if count == ne:
            target, target_k = jnp.int32(step), lax.rem(grp + step * nk // ne + turn, nk)
        else:
            target, target_k = lax.rem(step + count * grp, ne), grp
        src = coupled.at[:, pl.ds(tile * ROWS, ROWS), pl.ds(pl.multiple_of(grp * group, 128), group)]
        dst = recv.at[turn, my_e, my_k]
        own = (target == my_e) & (target_k == my_k)

        @pl.when(jnp.logical_not(own))
        def _():
            copy = pltpu.make_async_remote_copy(
                src_ref=src, dst_ref=dst, send_sem=in_send, recv_sem=in_recv.at[turn],
                device_id=(target, target_k), device_id_type=MESH,
            )
            if start:
                copy.start()
            else:
                copy.wait_send()

        if start:
            @pl.when(own)
            def _():
                pltpu.make_async_copy(src, dst, in_recv.at[turn]).start()

    def couple(grp, index):
        base = pl.multiple_of(jnp.clip((grp - 1) * group, 0, atoms - window), 128)
        index = index - base
        source = green[:, :, pl.ds(base, window)].reshape(block_rows * pairs, window)
        places = lax.broadcasted_iota(jnp.int32, (window, group), 0)
        for first in range(0, slots, 2):
            hits = [
                jnp.where(places == index[slot : slot + 1, :], 1.0, 0.0).astype(jnp.bfloat16)
                for slot in (first, first + 1)
            ]
            got = jnp.dot(
                source, jnp.concatenate(hits, axis=1), preferred_element_type=jnp.float32
            ).astype(jnp.bfloat16)
            for slot in (first, first + 1):
                for row in range(block_rows):
                    taken[slot * pairs : (slot + 1) * pairs, row * group : (row + 1) * group] = got[
                        row * pairs : (row + 1) * pairs,
                        (slot - first) * group : (slot - first + 1) * group,
                    ]
        total = jnp.dot(maps[...], taken[...], preferred_element_type=jnp.float32).astype(jnp.bfloat16)
        lanes = pl.ds(pl.multiple_of(grp * group, 128), group)
        for row in range(block_rows):
            coupled[row, :, lanes] = total[:, row * group : (row + 1) * group]

    early = tiles if rounds == 1 else EARLY

    def send_early(grp):
        for tile in range(early):
            in_copies(tile, grp, True)

    SCOPE("lgreen", lambda: [load.wait() for load in loads[2:]])
    SCOPE("couple0", lambda: couple(my_k, near[...]))
    SCOPE("small", lambda: fill_wide(small_kernel(phonon, offsets, block_rows), wide))
    SCOPE("barwait", lambda: pl.semaphore_wait(barrier, ne * nk - 1))
    all_others(lambda i: near_copy(i).start())
    send_early(my_k)

    def couple_other(i, _):
        grp = paired(my_k, i, nk)
        pltpu.make_async_remote_copy(
            src_ref=near, dst_ref=near_all.at[grp], send_sem=near_send, recv_sem=near_recv.at[grp],
            device_id=(my_e, grp), device_id_type=MESH,
        ).wait_recv()
        couple(grp, near_all[grp])
        send_early(grp)
        return 0

    SCOPE("couples", lambda: lax.fori_loop(1, nk, couple_other, 0))

    def send_late(i, _):
        grp = paired(my_k, i, nk)
        for tile in range(early, tiles):
            in_copies(tile, grp, True)
        return 0

    SCOPE("late", lambda: lax.fori_loop(0, nk, send_late, 0))

    def mine(turn):
        count = min(ne, tiles - turn * ne)
        if count == ne:
            return my_e, lax.rem(my_k + 2 * nk - lax.div(my_e * nk, ne) - turn, nk)
        return lax.rem(my_e + count * (ne - 1) * my_k, ne), my_k

    def out_copies(turn, start, places=tuple(range(ne))):
        step_of, grp_of = mine(turn)
        tile = step_of + turn * ne
        dst = out.at[
            :, pl.ds(pl.multiple_of(tile * ROWS, ROWS), ROWS), pl.ds(pl.multiple_of(grp_of * group, 128), group)
        ]

        def step(i, _):
            target = paired(my_k, i, nk)
            for other in places:
                src = res.at[turn, other, target]
                own = (other == my_e) & (target == my_k)

                @pl.when(jnp.logical_not(own))
                def _(src=src, other=other):
                    copy = pltpu.make_async_remote_copy(
                        src_ref=src, dst_ref=dst, send_sem=out_send, recv_sem=out_recv,
                        device_id=(jnp.int32(other), target), device_id_type=MESH,
                    )
                    if start:
                        copy.start()
                    else:
                        copy.wait_send()

                if start:
                    @pl.when(own)
                    def _(src=src):
                        pltpu.make_async_copy(src, dst, out_recv).start()
            return 0

        lax.fori_loop(0, nk, step, 0)

    def finish(turn):
        SCOPE("turnwait%d" % turn, lambda: pltpu.make_async_copy(recv.at[turn], recv.at[turn], in_recv.at[turn]).wait())
        span = flat * ROWS
        for place in range(ne):
            low, high = max(place - 1, 0), min(place + 1, ne - 1)
            piece = recv[turn, low : high + 1].reshape((high - low + 1) * span, group)
            value = jnp.dot(
                wide[:, (low - place + 1) * span : (high - place + 2) * span],
                piece,
                preferred_element_type=jnp.float32,
            )
            res[turn, place] = value.astype(jnp.bfloat16).reshape(nk, block_rows, ROWS, group)
            out_copies(turn, True, (place,))

    def each_turn(act):
        for turn in range(rounds):
            if turn * ne + ne <= tiles:
                act(turn)
            else:
                @pl.when(mine(turn)[0] + turn * ne < tiles)
                def _(turn=turn):
                    act(turn)

    each_turn(finish)

    def all_sent(block, sem, others):
        span = block.at[pl.ds(0, others)]
        pltpu.make_async_copy(span, span, sem).wait()

    def drain(turn):
        blocks = recv.at[turn]
        pltpu.make_async_copy(blocks.at[pl.ds(0, ne - 1)], blocks.at[pl.ds(0, ne - 1)], out_send).wait()
        all_sent(blocks.at[0], out_send, nk - 1)

    SCOPE("outwait", lambda: pltpu.make_async_copy(out, out, out_recv).wait())

    def finals():
        each_turn(drain)
        all_sent(near_all, near_send, nk - 1)
        for turn in range(rounds):
            count = min(ne, tiles - turn * ne)
            owner = mine(turn)[0] < count
            rows = nk * count
            full, rest = rows // nk, rows % nk
            first = recv.at[turn, pl.ds(0, count - 1)]
            if count > 1:
                pltpu.make_async_copy(first, first, in_send).wait()
            all_sent(recv.at[turn, 0], in_send, nk - 1)

            @pl.when(jnp.logical_not(owner))
            def _(turn=turn):
                all_sent(recv.at[turn, 0], in_send, 1)

    SCOPE("finals", finals)


def body(ne, nk, green_blocks, phonon, offsets, neighbours, coupling):
    block_rows, _, pairs, atoms = green_blocks.shape
    group, slots = neighbours.shape
    rounds = -(-(pairs // ROWS) // ne)
    window = min(3 * group, atoms)
    flat = nk * block_rows
    vmem = pl.BlockSpec(memory_space=pltpu.VMEM)
    anyw = pl.BlockSpec(memory_space=pl.ANY)
    ones = spread_ones(slots, coupling.shape[1])
    maps_in = coupling.transpose(1, 0, 2)
    block = (block_rows, ROWS, group)
    result = pl.pallas_call(
        functools.partial(kernel, (ne, nk, window)),
        out_shape=pltpu.VMEM((block_rows, pairs, atoms), jnp.bfloat16),
        in_specs=[anyw] * 6,
        out_specs=vmem,
        scratch_shapes=[
            pltpu.VMEM((block_rows, pairs, atoms), jnp.bfloat16),
            pltpu.VMEM((slots, group), jnp.int32),
            pltpu.VMEM(phonon.shape, jnp.float32),
            pltpu.SMEM(offsets.shape, jnp.int32),
            pltpu.VMEM(maps_in.shape, jnp.float32),
            pltpu.VMEM(ones.shape, jnp.bfloat16),
            pltpu.VMEM((pairs, slots * pairs), jnp.float32),
            pltpu.VMEM((pairs, slots * pairs), jnp.bfloat16),
            pltpu.VMEM((nk, slots, group), jnp.int32),
            pltpu.VMEM((slots * pairs, block_rows * group), jnp.bfloat16),
            pltpu.VMEM((block_rows, pairs, atoms), jnp.bfloat16),
            pltpu.VMEM((flat * ROWS, 3 * flat * ROWS), jnp.bfloat16),
            pltpu.VMEM((rounds, ne, nk) + block, jnp.bfloat16),
            pltpu.VMEM((rounds, ne, nk) + block, jnp.bfloat16),
            pltpu.SemaphoreType.DMA((6,)),
            pltpu.SemaphoreType.DMA,
            pltpu.SemaphoreType.DMA((nk,)),
            pltpu.SemaphoreType.DMA,
            pltpu.SemaphoreType.DMA((rounds,)),
            pltpu.SemaphoreType.DMA,
            pltpu.SemaphoreType.DMA,
        ],
        compiler_params=pltpu.CompilerParams(collective_id=0, has_side_effects=True),
    )(
        green_blocks.reshape(block_rows, pairs, atoms),
        neighbours.T,
        phonon,
        offsets,
        maps_in,
        ones,
    )
    return result.reshape(green_blocks.shape)


def solution(mesh):
    placed = (P("energy", "kmom", None, None), P(), P(), P("kmom", None), P())
    return jax.shard_map(
        functools.partial(body, mesh.shape["energy"], mesh.shape["kmom"]),
        mesh=mesh, in_specs=placed, out_specs=P("energy", "kmom", None, None), check_vma=False,
    )
```

```python
import functools

import jax
import jax.numpy as jnp
import numpy as np
from jax import lax
from jax.experimental import pallas as pl
from jax.experimental.pallas import tpu as pltpu
from jax.sharding import PartitionSpec as P

OFFSET = 2
RADIUS = 32
ROWS = 16
EARLY = 7
UNROLL = True
MESH = pl.DeviceIdType.MESH


def fill_ones(orbs, ones):
    height, count = ones.shape[0], ones.shape[1] // 2
    row = lax.broadcasted_iota(jnp.int32, (height, count), 0)
    col = lax.broadcasted_iota(jnp.int32, (height, count), 1)
    ahead = col - orbs * row
    ones[:, :count] = jnp.where((ahead >= 0) & (ahead < orbs), 1.0, 0.0).astype(jnp.bfloat16)
    line = lax.broadcasted_iota(jnp.int32, (height, 1), 0)
    slot = lax.div(line, orbs)
    ahead = col - (orbs * orbs * slot + line - orbs * slot)
    turns = jnp.floor((ahead.astype(jnp.float32) + 0.5) * (1.0 / orbs)) * orbs
    hit = (ahead >= 0) & (ahead < orbs * orbs) & (turns == ahead.astype(jnp.float32))
    ones[:, count:] = jnp.where(hit, 1.0, 0.0).astype(jnp.bfloat16)


def fill_maps(coupling, ones, maps_wide, maps):
    orbs, slots = coupling.shape[0], coupling.shape[1]
    count = slots * orbs * orbs
    blocks = jnp.concatenate([coupling[:, slot, :] for slot in range(slots)], axis=1)
    high = blocks.astype(jnp.bfloat16)
    rest = blocks - high.astype(jnp.float32)
    mid = rest.astype(jnp.bfloat16)
    low = (rest - mid.astype(jnp.float32)).astype(jnp.bfloat16)
    both = sum(
        jnp.dot(term, ones[...], preferred_element_type=jnp.float32) for term in (high, mid, low)
    )
    left, right = both[:, :count], both[:, count:]
    for orb in range(orbs):
        maps_wide[orb * orbs : (orb + 1) * orbs, :] = left[orb : orb + 1, :] * right
    maps[...] = maps_wide[...].astype(jnp.bfloat16)


def small_kernel(phonon, offsets, block_rows):
    freqs, moms = phonon.shape[1], phonon.shape[2]
    flat = moms * block_rows
    place = lax.broadcasted_iota(jnp.int32, (freqs, moms), 0)
    shift = jnp.zeros((freqs, moms), jnp.int32)
    for freq in range(freqs):
        shift = jnp.where(place == freq, offsets[freq], shift)
    row = lax.broadcasted_iota(jnp.int32, (flat, 3 * flat), 0)
    col = lax.broadcasted_iota(jnp.int32, (flat, 3 * flat), 1)
    mom_diff = (row // block_rows - (col // block_rows) % moms + moms) % moms
    tile = (col >= flat).astype(jnp.int32) + (col >= 2 * flat).astype(jnp.int32)
    rel = block_rows * (tile - 1) + col % block_rows - row % block_rows
    small = jnp.zeros((flat, 3 * flat), jnp.float32)
    for step in range(-OFFSET, OFFSET + 1):
        terms = [
            jnp.where((2 * sign - 1) * shift == step, phonon[sign], 0.0) for sign in (0, 1)
        ]
        taps = jnp.sum(terms[0] + terms[1], axis=0, keepdims=True)
        code = jnp.where(rel == step, mom_diff, -1)
        for mom in range(moms):
            small = jnp.where(code == mom, taps[:, mom : mom + 1], small)
    return small.astype(jnp.bfloat16)


def fill_wide(small, wide):
    flat = small.shape[0]
    grow = (
        lax.broadcasted_iota(jnp.int32, (flat * ROWS, flat), 0) // ROWS
        == lax.broadcasted_iota(jnp.int32, (flat * ROWS, flat), 1)
    )
    tall = jnp.dot(
        jnp.where(grow, 1.0, 0.0).astype(jnp.bfloat16), small, preferred_element_type=jnp.float32
    ).astype(jnp.bfloat16)
    for part in range(3):
        span = flat * ROWS
        spread = (
            lax.broadcasted_iota(jnp.int32, (flat, span), 1) // ROWS
            == lax.broadcasted_iota(jnp.int32, (flat, span), 0)
        )
        full = jnp.dot(
            tall[:, part * flat : (part + 1) * flat],
            jnp.where(spread, 1.0, 0.0).astype(jnp.bfloat16),
            preferred_element_type=jnp.float32,
        )
        same = (
            lax.broadcasted_iota(jnp.int32, (span, span), 0) % ROWS
            == lax.broadcasted_iota(jnp.int32, (span, span), 1) % ROWS
        )
        wide[:, part * span : (part + 1) * span] = jnp.where(same, full, 0.0).astype(jnp.bfloat16)


def SCOPE(name, act):
    with jax.named_scope(name):
        act()


def paired(index, step, count):
    if count & (count - 1):
        return lax.rem(index + step, count)
    total = jnp.int32(0)
    bit = 1
    while bit < count:
        total = total + lax.rem(lax.div(index, bit) + lax.div(step, bit), 2) * bit
        bit *= 2
    return total


def kernel(
    sizes, green_any, near_any, phonon_any, offsets_any, coupling_any, out,
    green, near, phonon, offsets, coupling, ones, maps_wide, maps, near_all, taken, coupled, wide, recv, res,
    load_sem, near_send, near_recv, in_send, in_recv, out_send, out_recv,
):
    ne, nk, window = sizes
    block_rows, pairs, atoms = green.shape
    slots, group = near.shape
    tiles = pairs // ROWS
    rounds = recv.shape[0]
    my_e = lax.axis_index("energy")
    my_k = lax.axis_index("kmom")

    barrier = pltpu.get_barrier_semaphore()
    loads = [
        pltpu.make_async_copy(src, dst, load_sem.at[i])
        for i, (src, dst) in enumerate(
            [
                (coupling_any, coupling), (near_any, near), (green_any, green),
                (phonon_any, phonon), (offsets_any, offsets),
            ]
        )
    ]
    for load in loads[:3]:
        load.start()

    def greet(i, _):
        place = lax.rem(my_e * nk + my_k + i, ne * nk)
        pl.semaphore_signal(
            barrier, inc=1, device_id=(lax.div(place, nk), lax.rem(place, nk)), device_id_type=MESH
        )
        return 0

    def greet_all():
        for step_e in range(ne):
            other_e = lax.rem(my_e + step_e, ne)
            for step_k in range(nk):
                if step_e or step_k:
                    pl.semaphore_signal(
                        barrier, inc=1, device_id=(other_e, lax.rem(my_k + step_k, nk)), device_id_type=MESH
                    )

    SCOPE("greet", greet_all)
    for load in loads[3:]:
        load.start()
    SCOPE("lones", lambda: fill_ones(coupling.shape[0], ones))
    SCOPE("lcoup", lambda: loads[0].wait())
    SCOPE("maps", lambda: fill_maps(coupling, ones, maps_wide, maps))
    flat = nk * block_rows

    def near_copy(i):
        other = paired(my_k, i, nk)
        return pltpu.make_async_remote_copy(
            src_ref=near, dst_ref=near_all.at[my_k], send_sem=near_send, recv_sem=near_recv.at[my_k],
            device_id=(my_e, other), device_id_type=MESH,
        )

    def all_others(act):
        def step(i, _):
            act(i)
            return 0

        lax.fori_loop(1, nk, step, 0)

    full = tiles // ne

    def send_tiles(grp, first, last):
        lanes = pl.ds(pl.multiple_of(grp * group, 128), group)

        def parts(tile):
            turn, step = tile // ne, tile % ne
            count = min(ne, tiles - turn * ne)
            if count == ne:
                target, target_k = jnp.int32(step), lax.rem(grp + step * nk // ne + turn, nk)
            else:
                target, target_k = lax.rem(step + count * grp, ne), grp
            src = coupled.at[:, pl.ds(tile * ROWS, ROWS), lanes]
            dst = recv.at[turn, my_e, my_k]

            def remote():
                pltpu.make_async_remote_copy(
                    src_ref=src, dst_ref=dst, send_sem=in_send, recv_sem=in_recv.at[turn],
                    device_id=(target, target_k), device_id_type=MESH,
                ).start()

            def local():
                pltpu.make_async_copy(src, dst, in_recv.at[turn]).start()

            return (target == my_e) & (target_k == my_k), remote, local

        every = [parts(tile) for tile in range(first, last)]
        ahead = lax.rem(my_k - grp - my_e * nk // ne + 2 * nk, nk)
        mixed = (ahead < full) | (grp == my_k)

        @pl.when(jnp.logical_not(mixed))
        def _():
            for _, remote, _ in every:
                remote()

        @pl.when(mixed)
        def _():
            for own, remote, local in every:
                pl.when(jnp.logical_not(own))(remote)
                pl.when(own)(local)

    def couple(grp, index):
        base = pl.multiple_of(jnp.clip((grp - 1) * group, 0, atoms - window), 128)
        index = index - base
        source = green[:, :, pl.ds(base, window)].reshape(block_rows * pairs, window)
        places = lax.broadcasted_iota(jnp.int32, (window, group), 0)
        for first in range(0, slots, 2):
            hits = [
                jnp.where(places == index[slot : slot + 1, :], 1.0, 0.0).astype(jnp.bfloat16)
                for slot in (first, first + 1)
            ]
            got = jnp.dot(
                source, jnp.concatenate(hits, axis=1), preferred_element_type=jnp.float32
            ).astype(jnp.bfloat16)
            for slot in (first, first + 1):
                for row in range(block_rows):
                    taken[slot * pairs : (slot + 1) * pairs, row * group : (row + 1) * group] = got[
                        row * pairs : (row + 1) * pairs,
                        (slot - first) * group : (slot - first + 1) * group,
                    ]
        total = jnp.dot(maps[...], taken[...], preferred_element_type=jnp.float32).astype(jnp.bfloat16)
        lanes = pl.ds(pl.multiple_of(grp * group, 128), group)
        for row in range(block_rows):
            coupled[row, :, lanes] = total[:, row * group : (row + 1) * group]

    early = tiles if rounds == 1 else EARLY

    def send_early(grp):
        send_tiles(grp, 0, early)

    SCOPE("lgreen", lambda: [load.wait() for load in loads[1:]])
    SCOPE("couple0", lambda: couple(my_k, near[...]))
    SCOPE("barwait", lambda: pl.semaphore_wait(barrier, ne * nk - 1))
    all_others(lambda i: near_copy(i).start())
    send_early(my_k)

    def couple_other(i, _):
        grp = paired(my_k, i, nk)
        pltpu.make_async_remote_copy(
            src_ref=near, dst_ref=near_all.at[grp], send_sem=near_send, recv_sem=near_recv.at[grp],
            device_id=(my_e, grp), device_id_type=MESH,
        ).wait_recv()
        couple(grp, near_all[grp])
        send_early(grp)
        return 0

    SCOPE("couples", lambda: lax.fori_loop(1, nk, couple_other, 0))

    def send_late(i, _):
        grp = paired(my_k, i, nk)
        send_tiles(grp, early, tiles)
        return 0

    SCOPE("late", lambda: lax.fori_loop(0, nk, send_late, 0))

    SCOPE("small", lambda: fill_wide(small_kernel(phonon, offsets, block_rows), wide))

    def mine(turn):
        count = min(ne, tiles - turn * ne)
        if count == ne:
            return my_e, lax.rem(my_k + 2 * nk - lax.div(my_e * nk, ne) - turn, nk)
        return lax.rem(my_e + count * (ne - 1) * my_k, ne), my_k

    def send_out(turn, place, dst):
        def remote(target):
            pltpu.make_async_remote_copy(
                src_ref=res.at[turn, place, target], dst_ref=dst, send_sem=out_send, recv_sem=out_recv,
                device_id=(jnp.int32(place), target), device_id_type=MESH,
            ).start()

        def step(i, _):
            remote(paired(my_k, jnp.where((my_k // 2 + 1 == nk // 4) | (my_k // 2 == nk // 4), i, nk - i), nk))
            return 0

        @pl.when(my_e != place)
        def _():
            remote(my_k)

        @pl.when(my_e == place)
        def _():
            pltpu.make_async_copy(res.at[turn, place, my_k], dst, out_recv).start()

        lax.fori_loop(1, nk, step, 0, unroll=UNROLL)

    def finish(turn):
        SCOPE("turnwait%d" % turn, lambda: pltpu.make_async_copy(recv.at[turn], recv.at[turn], in_recv.at[turn]).wait())
        span = flat * ROWS
        step_of, grp_of = mine(turn)
        tile = step_of + turn * ne
        dst = out.at[
            :, pl.ds(pl.multiple_of(tile * ROWS, ROWS), ROWS), pl.ds(pl.multiple_of(grp_of * group, 128), group)
        ]
        for place in range(ne):
            low, high = max(place - 1, 0), min(place + 1, ne - 1)
            piece = recv[turn, low : high + 1].reshape((high - low + 1) * span, group)
            value = jnp.dot(
                wide[:, (low - place + 1) * span : (high - place + 2) * span],
                piece,
                preferred_element_type=jnp.float32,
            )
            res[turn, place] = value.astype(jnp.bfloat16).reshape(nk, block_rows, ROWS, group)
            send_out(turn, place, dst)

    def each_turn(act):
        for turn in range(rounds):
            if turn * ne + ne <= tiles:
                act(turn)
            else:
                @pl.when(mine(turn)[0] + turn * ne < tiles)
                def _(turn=turn):
                    act(turn)

    each_turn(finish)

    def all_sent(block, sem, others):
        span = block.at[pl.ds(0, others)]
        pltpu.make_async_copy(span, span, sem).wait()

    def drain(turn):
        blocks = recv.at[turn]
        pltpu.make_async_copy(blocks.at[pl.ds(0, ne - 1)], blocks.at[pl.ds(0, ne - 1)], out_send).wait()
        all_sent(blocks.at[0], out_send, nk - 1)

    SCOPE("outwait", lambda: pltpu.make_async_copy(out, out, out_recv).wait())

    def finals():
        each_turn(drain)
        all_sent(near_all, near_send, nk - 1)
        for turn in range(rounds):
            count = min(ne, tiles - turn * ne)
            owner = mine(turn)[0] < count
            rows = nk * count
            full, rest = rows // nk, rows % nk
            first = recv.at[turn, pl.ds(0, count - 1)]
            if count > 1:
                pltpu.make_async_copy(first, first, in_send).wait()
            all_sent(recv.at[turn, 0], in_send, nk - 1)

            @pl.when(jnp.logical_not(owner))
            def _(turn=turn):
                all_sent(recv.at[turn, 0], in_send, 1)

    SCOPE("finals", finals)


def body(ne, nk, green_blocks, phonon, offsets, neighbours, coupling):
    block_rows, _, pairs, atoms = green_blocks.shape
    group, slots = neighbours.shape
    rounds = -(-(pairs // ROWS) // ne)
    window = min(3 * group, atoms)
    flat = nk * block_rows
    vmem = pl.BlockSpec(memory_space=pltpu.VMEM)
    anyw = pl.BlockSpec(memory_space=pl.ANY)
    maps_in = coupling.transpose(1, 0, 2)
    block = (block_rows, ROWS, group)
    result = pl.pallas_call(
        functools.partial(kernel, (ne, nk, window)),
        out_shape=pltpu.VMEM((block_rows, pairs, atoms), jnp.bfloat16),
        in_specs=[anyw] * 5,
        out_specs=vmem,
        scratch_shapes=[
            pltpu.VMEM((block_rows, pairs, atoms), jnp.bfloat16),
            pltpu.VMEM((slots, group), jnp.int32),
            pltpu.VMEM(phonon.shape, jnp.float32),
            pltpu.SMEM(offsets.shape, jnp.int32),
            pltpu.VMEM(maps_in.shape, jnp.float32),
            pltpu.VMEM((slots * coupling.shape[1], 2 * slots * pairs), jnp.bfloat16),
            pltpu.VMEM((pairs, slots * pairs), jnp.float32),
            pltpu.VMEM((pairs, slots * pairs), jnp.bfloat16),
            pltpu.VMEM((nk, slots, group), jnp.int32),
            pltpu.VMEM((slots * pairs, block_rows * group), jnp.bfloat16),
            pltpu.VMEM((block_rows, pairs, atoms), jnp.bfloat16),
            pltpu.VMEM((flat * ROWS, 3 * flat * ROWS), jnp.bfloat16),
            pltpu.VMEM((rounds, ne, nk) + block, jnp.bfloat16),
            pltpu.VMEM((rounds, ne, nk) + block, jnp.bfloat16),
            pltpu.SemaphoreType.DMA((5,)),
            pltpu.SemaphoreType.DMA,
            pltpu.SemaphoreType.DMA((nk,)),
            pltpu.SemaphoreType.DMA,
            pltpu.SemaphoreType.DMA((rounds,)),
            pltpu.SemaphoreType.DMA,
            pltpu.SemaphoreType.DMA,
        ],
        compiler_params=pltpu.CompilerParams(collective_id=0, has_side_effects=True),
    )(
        green_blocks.reshape(block_rows, pairs, atoms),
        neighbours.T,
        phonon,
        offsets,
        maps_in,
    )
    return result.reshape(green_blocks.shape)


def solution(mesh):
    placed = (P("energy", "kmom", None, None), P(), P(), P("kmom", None), P())
    return jax.shard_map(
        functools.partial(body, mesh.shape["energy"], mesh.shape["kmom"]),
        mesh=mesh, in_specs=placed, out_specs=P("energy", "kmom", None, None), check_vma=False,
    )
```

```python
import functools

import jax
import jax.numpy as jnp
import numpy as np
from jax import lax
from jax.experimental import pallas as pl
from jax.experimental.pallas import tpu as pltpu
from jax.sharding import PartitionSpec as P

OFFSET = 2
RADIUS = 32
ROWS = 16
EARLY = 7
UNROLL = True
MESH = pl.DeviceIdType.MESH


def fill_ones(orbs, ones):
    height, count = ones.shape[0], ones.shape[1] // 2
    row = lax.broadcasted_iota(jnp.int32, (height, count), 0)
    col = lax.broadcasted_iota(jnp.int32, (height, count), 1)
    ahead = col - orbs * row
    ones[:, :count] = jnp.where((ahead >= 0) & (ahead < orbs), 1.0, 0.0).astype(jnp.bfloat16)
    line = lax.broadcasted_iota(jnp.int32, (height, 1), 0)
    slot = lax.div(line, orbs)
    ahead = col - (orbs * orbs * slot + line - orbs * slot)
    turns = jnp.floor((ahead.astype(jnp.float32) + 0.5) * (1.0 / orbs)) * orbs
    hit = (ahead >= 0) & (ahead < orbs * orbs) & (turns == ahead.astype(jnp.float32))
    ones[:, count:] = jnp.where(hit, 1.0, 0.0).astype(jnp.bfloat16)


def fill_maps(coupling, ones, maps_wide, maps):
    orbs, slots = coupling.shape[0], coupling.shape[1]
    count = slots * orbs * orbs
    blocks = jnp.concatenate([coupling[:, slot, :] for slot in range(slots)], axis=1)
    high = blocks.astype(jnp.bfloat16)
    rest = blocks - high.astype(jnp.float32)
    mid = rest.astype(jnp.bfloat16)
    low = (rest - mid.astype(jnp.float32)).astype(jnp.bfloat16)
    both = sum(
        jnp.dot(term, ones[...], preferred_element_type=jnp.float32) for term in (high, mid, low)
    )
    left, right = both[:, :count], both[:, count:]
    for orb in range(orbs):
        maps_wide[orb * orbs : (orb + 1) * orbs, :] = left[orb : orb + 1, :] * right
    maps[...] = maps_wide[...].astype(jnp.bfloat16)


def small_kernel(phonon, offsets, block_rows):
    freqs, moms = phonon.shape[1], phonon.shape[2]
    flat = moms * block_rows
    place = lax.broadcasted_iota(jnp.int32, (freqs, moms), 0)
    shift = jnp.zeros((freqs, moms), jnp.int32)
    for freq in range(freqs):
        shift = jnp.where(place == freq, offsets[freq], shift)
    row = lax.broadcasted_iota(jnp.int32, (flat, 3 * flat), 0)
    col = lax.broadcasted_iota(jnp.int32, (flat, 3 * flat), 1)
    mom_diff = (row // block_rows - (col // block_rows) % moms + moms) % moms
    tile = (col >= flat).astype(jnp.int32) + (col >= 2 * flat).astype(jnp.int32)
    rel = block_rows * (tile - 1) + col % block_rows - row % block_rows
    small = jnp.zeros((flat, 3 * flat), jnp.float32)
    for step in range(-OFFSET, OFFSET + 1):
        terms = [
            jnp.where((2 * sign - 1) * shift == step, phonon[sign], 0.0) for sign in (0, 1)
        ]
        taps = jnp.sum(terms[0] + terms[1], axis=0, keepdims=True)
        code = jnp.where(rel == step, mom_diff, -1)
        for mom in range(moms):
            small = jnp.where(code == mom, taps[:, mom : mom + 1], small)
    return small.astype(jnp.bfloat16)


def fill_wide(small, wide):
    flat = small.shape[0]
    grow = (
        lax.broadcasted_iota(jnp.int32, (flat * ROWS, flat), 0) // ROWS
        == lax.broadcasted_iota(jnp.int32, (flat * ROWS, flat), 1)
    )
    tall = jnp.dot(
        jnp.where(grow, 1.0, 0.0).astype(jnp.bfloat16), small, preferred_element_type=jnp.float32
    ).astype(jnp.bfloat16)
    for part in range(3):
        span = flat * ROWS
        spread = (
            lax.broadcasted_iota(jnp.int32, (flat, span), 1) // ROWS
            == lax.broadcasted_iota(jnp.int32, (flat, span), 0)
        )
        full = jnp.dot(
            tall[:, part * flat : (part + 1) * flat],
            jnp.where(spread, 1.0, 0.0).astype(jnp.bfloat16),
            preferred_element_type=jnp.float32,
        )
        same = (
            lax.broadcasted_iota(jnp.int32, (span, span), 0) % ROWS
            == lax.broadcasted_iota(jnp.int32, (span, span), 1) % ROWS
        )
        wide[:, part * span : (part + 1) * span] = jnp.where(same, full, 0.0).astype(jnp.bfloat16)


def SCOPE(name, act):
    with jax.named_scope(name):
        act()


def paired(index, step, count):
    if count & (count - 1):
        return lax.rem(index + step, count)
    total = jnp.int32(0)
    bit = 1
    while bit < count:
        total = total + lax.rem(lax.div(index, bit) + lax.div(step, bit), 2) * bit
        bit *= 2
    return total


def kernel(
    sizes, green_any, near_any, phonon_any, offsets_any, coupling_any, out,
    green, near, phonon, offsets, coupling, ones, maps_wide, maps, near_all, taken, coupled, wide, recv, res,
    load_sem, near_send, near_recv, in_send, in_recv, out_send, out_recv,
):
    ne, nk, window = sizes
    block_rows, pairs, atoms = green.shape
    slots, group = near.shape
    tiles = pairs // ROWS
    rounds = recv.shape[0]
    my_e = lax.axis_index("energy")
    my_k = lax.axis_index("kmom")

    barrier = pltpu.get_barrier_semaphore()
    loads = [
        pltpu.make_async_copy(src, dst, load_sem.at[i])
        for i, (src, dst) in enumerate(
            [
                (coupling_any, coupling), (near_any, near), (green_any, green),
                (phonon_any, phonon), (offsets_any, offsets),
            ]
        )
    ]
    for load in loads[:3]:
        load.start()

    def greet(i, _):
        place = lax.rem(my_e * nk + my_k + i, ne * nk)
        pl.semaphore_signal(
            barrier, inc=1, device_id=(lax.div(place, nk), lax.rem(place, nk)), device_id_type=MESH
        )
        return 0

    def greet_all():
        for step_e in range(ne):
            other_e = lax.rem(my_e + step_e, ne)
            for step_k in range(nk):
                if step_e or step_k:
                    pl.semaphore_signal(
                        barrier, inc=1, device_id=(other_e, lax.rem(my_k + step_k, nk)), device_id_type=MESH
                    )

    SCOPE("greet", greet_all)
    for load in loads[3:]:
        load.start()
    SCOPE("lones", lambda: fill_ones(coupling.shape[0], ones))
    SCOPE("lcoup", lambda: loads[0].wait())
    SCOPE("maps", lambda: fill_maps(coupling, ones, maps_wide, maps))
    flat = nk * block_rows

    def near_copy(i):
        other = paired(my_k, i, nk)
        return pltpu.make_async_remote_copy(
            src_ref=near, dst_ref=near_all.at[my_k], send_sem=near_send, recv_sem=near_recv.at[my_k],
            device_id=(my_e, other), device_id_type=MESH,
        )

    def all_others(act):
        def step(i, _):
            act(i)
            return 0

        lax.fori_loop(1, nk, step, 0)

    full = tiles // ne

    def send_tiles(grp, first, last):
        lanes = pl.ds(pl.multiple_of(grp * group, 128), group)

        def parts(tile):
            turn, step = tile // ne, tile % ne
            count = min(ne, tiles - turn * ne)
            if count == ne:
                target, target_k = jnp.int32(step), lax.rem(grp + step * nk // ne + turn, nk)
            else:
                target, target_k = lax.rem(step + count * grp, ne), grp
            src = coupled.at[:, pl.ds(tile * ROWS, ROWS), lanes]
            dst = recv.at[turn, my_e, my_k]

            def remote():
                pltpu.make_async_remote_copy(
                    src_ref=src, dst_ref=dst, send_sem=in_send, recv_sem=in_recv.at[turn],
                    device_id=(target, target_k), device_id_type=MESH,
                ).start()

            def local():
                pltpu.make_async_copy(src, dst, in_recv.at[turn]).start()

            return (target == my_e) & (target_k == my_k), remote, local

        every = [parts(tile) for tile in range(first, last)]
        ahead = lax.rem(my_k - grp - my_e * nk // ne + 2 * nk, nk)
        mixed = (ahead < full) | (grp == my_k)

        @pl.when(jnp.logical_not(mixed))
        def _():
            for _, remote, _ in every:
                remote()

        @pl.when(mixed)
        def _():
            for own, remote, local in every:
                pl.when(jnp.logical_not(own))(remote)
                pl.when(own)(local)

    def couple(grp, index):
        base = pl.multiple_of(jnp.clip((grp - 1) * group, 0, atoms - window), 128)
        index = index - base
        source = green[:, :, pl.ds(base, window)].reshape(block_rows * pairs, window)
        places = lax.broadcasted_iota(jnp.int32, (window, group), 0)
        for first in range(0, slots, 2):
            hits = [
                jnp.where(places == index[slot : slot + 1, :], 1.0, 0.0).astype(jnp.bfloat16)
                for slot in (first, first + 1)
            ]
            got = jnp.dot(
                source, jnp.concatenate(hits, axis=1), preferred_element_type=jnp.float32
            ).astype(jnp.bfloat16)
            for slot in (first, first + 1):
                for row in range(block_rows):
                    taken[slot * pairs : (slot + 1) * pairs, row * group : (row + 1) * group] = got[
                        row * pairs : (row + 1) * pairs,
                        (slot - first) * group : (slot - first + 1) * group,
                    ]
        total = jnp.dot(maps[...], taken[...], preferred_element_type=jnp.float32).astype(jnp.bfloat16)
        lanes = pl.ds(pl.multiple_of(grp * group, 128), group)
        for row in range(block_rows):
            coupled[row, :, lanes] = total[:, row * group : (row + 1) * group]

    early = tiles if rounds == 1 else EARLY

    def send_early(grp):
        send_tiles(grp, 0, early)

    SCOPE("lgreen", lambda: [load.wait() for load in loads[1:]])
    SCOPE("couple0", lambda: couple(my_k, near[...]))
    SCOPE("barwait", lambda: pl.semaphore_wait(barrier, ne * nk - 1))
    all_others(lambda i: near_copy(i).start())
    send_early(my_k)

    def couple_other(i, _):
        grp = paired(my_k, i, nk)
        pltpu.make_async_remote_copy(
            src_ref=near, dst_ref=near_all.at[grp], send_sem=near_send, recv_sem=near_recv.at[grp],
            device_id=(my_e, grp), device_id_type=MESH,
        ).wait_recv()
        couple(grp, near_all[grp])
        send_early(grp)
        return 0

    SCOPE("couples", lambda: lax.fori_loop(1, nk, couple_other, 0))

    def send_late(i, _):
        grp = paired(my_k, nk - 1 - i, nk)
        send_tiles(grp, early, tiles)
        return 0

    SCOPE("late", lambda: lax.fori_loop(0, nk, send_late, 0))

    SCOPE("small", lambda: fill_wide(small_kernel(phonon, offsets, block_rows), wide))

    def mine(turn):
        count = min(ne, tiles - turn * ne)
        if count == ne:
            return my_e, lax.rem(my_k + 2 * nk - lax.div(my_e * nk, ne) - turn, nk)
        return lax.rem(my_e + count * (ne - 1) * my_k, ne), my_k

    def send_out(turn, place, dst):
        def remote(target):
            pltpu.make_async_remote_copy(
                src_ref=res.at[turn, place, target], dst_ref=dst, send_sem=out_send, recv_sem=out_recv,
                device_id=(jnp.int32(place), target), device_id_type=MESH,
            ).start()

        def step(i, _):
            remote(paired(my_k, jnp.where((my_k // 2 + 1 == nk // 4) | (my_k // 2 == nk // 4), i, nk - i), nk))
            return 0

        @pl.when(my_e != place)
        def _():
            remote(my_k)

        @pl.when(my_e == place)
        def _():
            pltpu.make_async_copy(res.at[turn, place, my_k], dst, out_recv).start()

        lax.fori_loop(1, nk, step, 0, unroll=UNROLL)

    def finish(turn):
        SCOPE("turnwait%d" % turn, lambda: pltpu.make_async_copy(recv.at[turn], recv.at[turn], in_recv.at[turn]).wait())
        span = flat * ROWS
        step_of, grp_of = mine(turn)
        tile = step_of + turn * ne
        dst = out.at[
            :, pl.ds(pl.multiple_of(tile * ROWS, ROWS), ROWS), pl.ds(pl.multiple_of(grp_of * group, 128), group)
        ]
        for place in range(ne):
            low, high = max(place - 1, 0), min(place + 1, ne - 1)
            piece = recv[turn, low : high + 1].reshape((high - low + 1) * span, group)
            value = jnp.dot(
                wide[:, (low - place + 1) * span : (high - place + 2) * span],
                piece,
                preferred_element_type=jnp.float32,
            )
            res[turn, place] = value.astype(jnp.bfloat16).reshape(nk, block_rows, ROWS, group)
            send_out(turn, place, dst)

    def each_turn(act):
        for turn in range(rounds):
            if turn * ne + ne <= tiles:
                act(turn)
            else:
                @pl.when(mine(turn)[0] + turn * ne < tiles)
                def _(turn=turn):
                    act(turn)

    each_turn(finish)

    def all_sent(block, sem, others):
        span = block.at[pl.ds(0, others)]
        pltpu.make_async_copy(span, span, sem).wait()

    def drain(turn):
        blocks = recv.at[turn]
        pltpu.make_async_copy(blocks.at[pl.ds(0, ne - 1)], blocks.at[pl.ds(0, ne - 1)], out_send).wait()
        all_sent(blocks.at[0], out_send, nk - 1)

    SCOPE("outwait", lambda: pltpu.make_async_copy(out, out, out_recv).wait())

    def finals():
        each_turn(drain)
        all_sent(near_all, near_send, nk - 1)
        for turn in range(rounds):
            count = min(ne, tiles - turn * ne)
            owner = mine(turn)[0] < count
            rows = nk * count
            full, rest = rows // nk, rows % nk
            first = recv.at[turn, pl.ds(0, count - 1)]
            if count > 1:
                pltpu.make_async_copy(first, first, in_send).wait()
            all_sent(recv.at[turn, 0], in_send, nk - 1)

            @pl.when(jnp.logical_not(owner))
            def _(turn=turn):
                all_sent(recv.at[turn, 0], in_send, 1)

    SCOPE("finals", finals)


def body(ne, nk, green_blocks, phonon, offsets, neighbours, coupling):
    block_rows, _, pairs, atoms = green_blocks.shape
    group, slots = neighbours.shape
    rounds = -(-(pairs // ROWS) // ne)
    window = min(3 * group, atoms)
    flat = nk * block_rows
    vmem = pl.BlockSpec(memory_space=pltpu.VMEM)
    anyw = pl.BlockSpec(memory_space=pl.ANY)
    maps_in = coupling.transpose(1, 0, 2)
    block = (block_rows, ROWS, group)
    result = pl.pallas_call(
        functools.partial(kernel, (ne, nk, window)),
        out_shape=pltpu.VMEM((block_rows, pairs, atoms), jnp.bfloat16),
        in_specs=[anyw] * 5,
        out_specs=vmem,
        scratch_shapes=[
            pltpu.VMEM((block_rows, pairs, atoms), jnp.bfloat16),
            pltpu.VMEM((slots, group), jnp.int32),
            pltpu.VMEM(phonon.shape, jnp.float32),
            pltpu.SMEM(offsets.shape, jnp.int32),
            pltpu.VMEM(maps_in.shape, jnp.float32),
            pltpu.VMEM((slots * coupling.shape[1], 2 * slots * pairs), jnp.bfloat16),
            pltpu.VMEM((pairs, slots * pairs), jnp.float32),
            pltpu.VMEM((pairs, slots * pairs), jnp.bfloat16),
            pltpu.VMEM((nk, slots, group), jnp.int32),
            pltpu.VMEM((slots * pairs, block_rows * group), jnp.bfloat16),
            pltpu.VMEM((block_rows, pairs, atoms), jnp.bfloat16),
            pltpu.VMEM((flat * ROWS, 3 * flat * ROWS), jnp.bfloat16),
            pltpu.VMEM((rounds, ne, nk) + block, jnp.bfloat16),
            pltpu.VMEM((rounds, ne, nk) + block, jnp.bfloat16),
            pltpu.SemaphoreType.DMA((5,)),
            pltpu.SemaphoreType.DMA,
            pltpu.SemaphoreType.DMA((nk,)),
            pltpu.SemaphoreType.DMA,
            pltpu.SemaphoreType.DMA((rounds,)),
            pltpu.SemaphoreType.DMA,
            pltpu.SemaphoreType.DMA,
        ],
        compiler_params=pltpu.CompilerParams(collective_id=0, has_side_effects=True),
    )(
        green_blocks.reshape(block_rows, pairs, atoms),
        neighbours.T,
        phonon,
        offsets,
        maps_in,
    )
    return result.reshape(green_blocks.shape)


def solution(mesh):
    placed = (P("energy", "kmom", None, None), P(), P(), P("kmom", None), P())
    return jax.shard_map(
        functools.partial(body, mesh.shape["energy"], mesh.shape["kmom"]),
        mesh=mesh, in_specs=placed, out_specs=P("energy", "kmom", None, None), check_vma=False,
    )
```
